128 devices in a mesh: ep: 16 (over y, z_hi, core), dp: 8 (over z_lo, x).
Axes of the slice: x: 4, y: 4, z: 4 (z_hi: 2, z_lo: 2; z = z_hi * 2 + z_lo), core: 2. Of those that a mesh axis runs over, the one named last changes fastest.
Arguments:
- tokens: bfloat16 [8192, 2048], P(('ep', 'dp')), may hold values from -6 to 6
- slot_route: int32 [8192, 8], P(('ep', 'dp')), may hold values from 0 to 127, all different within a row; in each aligned block of 64 rows (0 to 63, 64 to 127, ...) at most 6 rows name the same one
- route_gate: float32 [8192, 8], P(('ep', 'dp')), may hold values from 0.04 to 0.4
- placement_table: int32 [128], replicated, may hold values from 0 to 63, as said below
- refreshed: int32 [32], replicated, may hold values from 0 to 63, as said below
- slot_gate_up: bfloat16 [128, 2048, 1536], P(('ep', 'dp')), may hold values from -0.125 to 0.125
- slot_down: bfloat16 [128, 768, 2048], P(('ep', 'dp')), may hold values from -0.21875 to 0.21875
- new_gate_up: bfloat16 [32, 2048, 1536], P('ep', 'dp'), may hold values from -0.125 to 0.125
- new_down: bfloat16 [32, 768, 2048], P('ep', 'dp'), may hold values from -0.21875 to 0.21875
Outputs:
- mixed: bfloat16 [8192, 2048], P(('ep', 'dp'))
The draws below stay inside these ranges and needn't reach their ends.
Inputs may be any that keep to these rules, and one draw needn't show every extreme that they name: `placement_table`: slot s lives on device s of ep+dp (ep major); write s = c * 8 + m. Every expert has one slot or more. A slot with m < 6 serves a refreshed expert whose position r in refreshed has r // 2 = (c + f(m)) mod 16, where f(m) = m for m < 4, f(4) = 8 and f(5) = 15; a slot with m >= 6 serves an expert that is not refreshed. `refreshed`: distinct expert ids. `slot_route`: each row names 8 distinct slots. Among the 64 rows of one device no slot is named more than 6 times, a bound that some block reaches.
All inputs are finite; a program needn't handle non-finite values.
Results may differ from the reference program's by a relative error of at most 0.0057.
Values may be sent and summed in bfloat16 or wider, within the bound.
No kernel may reach another device: no remote copies, remote signals or barrier semaphores. Data moves between devices by JAX's collectives and lax.ppermute only.
A program may use at most 128 MiB of HBM per device.

```python
import math
import jax
import jax.numpy as jnp
import numpy as np
from jax import lax

D = 2048
FF = 768
TOP = 8
REF_EP = 2
TOK_DEV = 64
SLOTS = 128
REFRESH = 32
NREF_COL = 6
EXPERTS = 64
CAP = 6
TOKENS = 8192
N_EP = 16
N_DP = 8


def layout_tables(key):
    shuffled = jax.random.permutation(jax.random.fold_in(key, 11), EXPERTS).astype(jnp.int32)
    parity = jax.random.randint(jax.random.fold_in(key, 13), (N_EP,), 0, REF_EP)
    column = jnp.arange(N_EP, dtype=jnp.int32)[:, None]
    member = jnp.arange(N_DP, dtype=jnp.int32)[None, :]
    offsets = jnp.where(member < NREF_COL - 2, member, jnp.where(member == NREF_COL - 2, N_EP // 2, N_EP - 1))
    owners = (column + offsets) % N_EP
    ref_index = REF_EP * owners + (member + parity[owners]) % REF_EP
    later = column * (N_DP - NREF_COL) + jnp.maximum(member - NREF_COL, 0)
    layout = jnp.where(member < NREF_COL, shuffled[ref_index], shuffled[REFRESH + later])
    return (layout.reshape(-1).astype(jnp.int32), shuffled[:REFRESH])


def draw_placement_table(key, part):
    return layout_tables(key)[0]


def draw_refreshed(key, part):
    return layout_tables(key)[1]


def shard_levels(rng, extent, cuts, smallest, high):
    loudness, own = 1.0, jax.random.fold_in(rng, 6)
    for dim, parts in cuts:
        steps = jnp.exp(jax.random.uniform(jax.random.fold_in(own, dim), (parts,), jnp.float32, smallest / len(cuts), high / len(cuts)))
        loudness = loudness * jnp.repeat(steps, extent[dim] // parts).reshape([-1 if axis == dim else 1 for axis in range(len(extent))])
    return loudness


def routed_block(stream_key, own, number, rows, number_of, top, bound, lean):
    ranking = jax.random.permutation(stream_key, number_of)
    crowded, usual = portions_of(number_of, rows * top, bound, lean, True), portions_of(number_of, rows * top, bound, lean, False)
    places = jnp.arange(number_of)

    def named(lengths, rotation):
        used = int((lengths > 0).sum())
        fixed = max(1, used // 4)
        moved = fixed + (places - fixed + rotation * (used - fixed)) % max(1, number_of - fixed)
        return jnp.zeros((number_of,), jnp.int32).at[ranking[jnp.where(places < fixed, places, moved)]].set(jnp.asarray(lengths, jnp.int32))

    lengths = jnp.where(number % 4 == 0, named(crowded, number // 4), named(usual, number - number // 4 - 1))
    mixed = jax.random.permutation(jax.random.fold_in(own, 3), number_of)
    giver, taker = mixed[0:number_of // 2 * 2:2], mixed[1:number_of // 2 * 2:2]
    room = jnp.minimum(lengths[giver] - 1, bound - lengths[taker]) // 2
    room = jnp.where((giver == ranking[0]) | (taker == ranking[0]) | (lengths[taker] == 0), 0, jnp.maximum(room, 0))
    moved = jax.random.randint(jax.random.fold_in(own, 4), (number_of // 2,), 0, 1 << 20) % (room + 1)
    lengths = lengths.at[giver].add(-moved).at[taker].add(moved)
    items = jnp.searchsorted(jnp.cumsum(lengths), jnp.arange(rows * top), side="right").astype(jnp.int32)
    grid = items.reshape(top, rows).T
    grid = grid[jax.random.permutation(jax.random.fold_in(own, 1), rows)]
    rotation = jax.random.randint(jax.random.fold_in(own, 2), (rows, 1), 0, top)
    return jnp.take_along_axis(grid, (jnp.arange(top)[None, :] + rotation) % top, axis=1)


def portions_of(count, total, bound, lean, full):
    weights = [(1 << 20) // math.isqrt(standing ** lean) + 1 for standing in range(1, count + 1)]
    largest = bound if full else min(bound, max(-(-total // count), total * weights[0] // sum(weights)))
    least = 1 if total - largest >= count - 1 else 0
    counts, rest = [largest] + [least] * (count - 1), total - largest - least * (count - 1)
    while rest > 0:
        movable = [i for i in range(1, count) if counts[i] < largest] or [i for i in range(1, count) if counts[i] < bound]
        pool, left = sum([weights[i] for i in movable]), rest
        for i in movable:
            more = min(bound - counts[i], max(1, left * weights[i] // pool), rest)
            counts[i] = counts[i] + more
            rest = rest - more
    return np.array(counts)


def bell_draw(stream_key, dims, scale, most, split=(), held_as=jnp.bfloat16):
    loudness = shard_levels(stream_key, dims, split, -0.22, 0.18) if split else 1.0
    values = jax.random.normal(stream_key, dims, jnp.float32) * scale * loudness
    return jnp.minimum(jnp.maximum(values, -most), most).astype(held_as)


def setup_inputs(seed: int = 0) -> dict:
    key_list = jax.random.split(jax.random.key(seed), 10)
    tokens = bell_draw(key_list[0], (TOKENS, D), 1.0, 6.0, ((0, 128),))
    slot_route_keys = jax.random.split(jax.random.fold_in(key_list[1], 1), TOKENS // TOK_DEV)
    slot_route_turns = jax.random.permutation(jax.random.fold_in(key_list[1], 3), TOKENS // TOK_DEV)
    slot_route = jax.vmap(lambda own, number: routed_block(jax.random.fold_in(key_list[1], 2), own, number, TOK_DEV, SLOTS, TOP, CAP, 2))(slot_route_keys, slot_route_turns).reshape((TOKENS, TOP))
    route_gate = jnp.clip(jnp.exp(math.log(0.4) - 2.3025851 * jax.random.uniform(key_list[2], (TOKENS, TOP), jnp.float32) ** shard_levels(key_list[2], (TOKENS, TOP), ((0, 128),), -0.2, 0.2)), 0.04, 0.4)
    placement_table = draw_placement_table(jax.random.fold_in(key_list[9], 71), 0)
    refreshed = draw_refreshed(jax.random.fold_in(key_list[9], 71), 0)
    slot_gate_up = bell_draw(key_list[5], (SLOTS, D, 2 * FF), D ** -0.5, 0.125, ((0, 128),))
    slot_down = bell_draw(key_list[6], (SLOTS, FF, D), FF ** -0.5, 0.21875, ((0, 128),))
    new_gate_up = bell_draw(key_list[7], (REFRESH, D, 2 * FF), D ** -0.5, 0.125, ((0, 16), (1, 8)))
    new_down = bell_draw(key_list[8], (REFRESH, FF, D), FF ** -0.5, 0.21875, ((0, 16), (1, 8)))
    return {"tokens": tokens, "slot_route": slot_route, "route_gate": route_gate, "placement_table": placement_table, "refreshed": refreshed, "slot_gate_up": slot_gate_up, "slot_down": slot_down, "new_gate_up": new_gate_up, "new_down": new_down}


def slot_weights(slot, placement_table, refreshed, slot_gate_up, slot_down, new_gate_up, new_down):
    matches = refreshed == placement_table[slot]
    renewed = jnp.any(matches)
    which_one = jnp.sum(jnp.where(matches, jnp.arange(REFRESH, dtype=jnp.int32), 0)).astype(jnp.int32)
    weight_up = jnp.where(renewed, new_gate_up[which_one], slot_gate_up[slot])
    weight_down = jnp.where(renewed, new_down[which_one], slot_down[slot])
    return weight_up, weight_down


def reference(tokens, slot_route, route_gate, placement_table, refreshed, slot_gate_up, slot_down, new_gate_up, new_down):
    routes_flat = slot_route.reshape(-1).astype(jnp.int32)
    gates_flat = route_gate.reshape(-1)
    row_total = routes_flat.shape[0]
    most_rows = SLOTS * CAP

    def one_slot(slot, summed):
        weight_up, weight_down = slot_weights(slot, placement_table, refreshed, slot_gate_up, slot_down, new_gate_up, new_down)
        positions = jnp.nonzero(routes_flat == slot, size=most_rows, fill_value=row_total)[0].astype(jnp.int32)
        filled = positions < row_total
        safe = jnp.minimum(positions, row_total - 1).astype(jnp.int32)
        gathered = tokens[safe // TOP]
        projected = jnp.dot(gathered, weight_up, preferred_element_type=jnp.float32)
        hidden = (jax.nn.silu(projected[:, :FF]) * projected[:, FF:]).astype(jnp.bfloat16)
        expert_out = jnp.dot(hidden, weight_down, preferred_element_type=jnp.float32).astype(jnp.bfloat16)
        weights = jnp.where(filled, gates_flat[safe], jnp.zeros((), gates_flat.dtype))
        return summed.at[safe // TOP].add(weights[:, None] * expert_out.astype(summed.dtype))

    summed = lax.fori_loop(0, SLOTS, one_slot, jnp.zeros((TOKENS, D), jnp.float32))
    return summed.astype(jnp.bfloat16)
```

```python
import jax
import jax.numpy as jnp
from jax import lax
from jax.experimental import pallas as pl
from jax.experimental.pallas import tpu as pltpu
from jax.sharding import PartitionSpec as P

D = 2048
FF = 768
TOP = 8
CAP = 6
TOK = 64
SLOTS = 128
GROUPS = 16
MEMBERS = 8
ACTIVE = 6
SHIFT = (0, 1, 2, 3, 8, 15, 0, 0)
PACK = 8
WIDE = 1536
PART = 512
ROWS = SLOTS * PACK
DENSE = SLOTS * CAP


ANY = pl.BlockSpec(memory_space=pl.ANY)
SMEM = pl.BlockSpec(memory_space=pltpu.SMEM)
VMEM = pl.BlockSpec(memory_space=pltpu.VMEM)
F32 = jnp.float32
BF16 = jnp.bfloat16


def params():
    return pltpu.CompilerParams(vmem_limit_bytes=56 * 1024 * 1024)


def iota(shape, dim):
    return lax.broadcasted_iota(jnp.int32, shape, dim)


def nt_dot(a, b):
    return lax.dot_general(a, b, (((1,), (1,)), ((), ())), preferred_element_type=F32)


def nn_dot(a, b):
    return jnp.dot(a, b, preferred_element_type=F32)


def shift_of(member):
    return jnp.where(member < 4, member, jnp.where(member == 4, 8, jnp.where(member == 5, 15, 0)))


def home_of(slot):
    member = slot & 7
    return ((((slot >> 3) + shift_of(member)) & 15) << 3) | member


def ranks(route, gate):
    home = home_of(route)
    lanes = iota((TOK, SLOTS), 1)
    hits = jnp.zeros((TOK, SLOTS), F32)
    gates = jnp.zeros((TOK, SLOTS), F32)
    for k in range(TOP):
        hit = home[:, k : k + 1] == lanes
        hits = jnp.where(hit, 1.0, hits)
        if gate is not None:
            gates = jnp.where(hit, gate[:, k : k + 1], gates)
    lower = (iota((TOK, TOK), 0) > iota((TOK, TOK), 1)).astype(F32).astype(BF16)
    rank = nn_dot(lower, hits.astype(BF16))
    return jnp.where(hits > 0, rank, -1.0), gates


def spread():
    return ((iota((ROWS, SLOTS), 0) >> 3) == iota((ROWS, SLOTS), 1)).astype(F32).astype(BF16)


def stage_kernel(info, gu, dn, *refs):
    outs_gu, outs_dn = refs[0:7], refs[7:14]
    vgu, vdn, sem_in, sem_out = refs[14:]
    load_gu = pltpu.make_async_copy(gu, vgu, sem_in.at[0])
    load_dn = pltpu.make_async_copy(dn, vdn, sem_in.at[1])
    load_gu.start()
    load_dn.start()
    load_gu.wait()
    copies = []
    for k in range(1, 8):
        copies.append(pltpu.make_async_copy(vgu.at[info[k]], outs_gu[k - 1], sem_out.at[k - 1]))
        copies[-1].start()
    load_dn.wait()
    for k in range(1, 8):
        copies.append(pltpu.make_async_copy(vdn.at[info[k]], outs_dn[k - 1], sem_out.at[k + 6]))
        copies[-1].start()
    for c in copies:
        c.wait()


def dispatch_kernel(route, tokens, out):
    rank, _ = ranks(route[...], None)
    twice = jnp.concatenate([rank, rank], axis=0).astype(BF16)
    wide = nt_dot(spread(), twice)
    place = (iota((ROWS, SLOTS), 0) & 7).astype(F32)
    left = iota((ROWS, SLOTS), 1) < TOK
    main = left & (wide == place) & (place < CAP)
    for j in range(3):
        wanted = jnp.where(place == 6, float(j), jnp.where(place == 7, float(3 + j), -2.0))
        pick = (main | (jnp.logical_not(left) & (wide == wanted))).astype(F32).astype(BF16)
        rhs = jnp.concatenate([tokens[:, PART * j : PART * (j + 1)], tokens[:, WIDE:]], axis=0)
        out[:, PART * j : PART * (j + 1)] = nn_dot(pick, rhs).astype(BF16)


def compact_kernel(x, out):
    row = iota((96, 128), 0)
    col = iota((96, 128), 1)
    owner = row // 6
    rank = row - 6 * owner
    main = (col == 8 * owner + rank).astype(F32).astype(BF16)
    extra = []
    for j in range(3):
        hit = (col == 8 * owner + 6) & (rank == j) | (col == 8 * owner + 7) & (rank == 3 + j)
        extra.append(hit.astype(F32).astype(BF16))
    extra = jnp.concatenate(extra, axis=1)
    for b in range(8):
        blk = x[128 * b : 128 * (b + 1), :]
        out[96 * b : 96 * (b + 1), 0:WIDE] = nn_dot(main, blk).astype(BF16)
        tall = jnp.concatenate([blk[:, PART * j : PART * (j + 1)] for j in range(3)], axis=0)
        out[96 * b : 96 * (b + 1), WIDE:] = nn_dot(extra, tall).astype(BF16)


def up_kernel(info, x, own, *refs):
    got = refs[0:7]
    slot, out, wbuf, sem = refs[7:]
    member = info[8]
    active = member < ACTIVE
    tile = 256

    def fetch(i):
        buf = i % 2

        @pl.when(active)
        def _():
            for side in range(2):
                cols = pl.ds(side * FF + tile * i, tile)
                for k in range(8):
                    src = own.at[info[0], :, cols] if k == 0 else got[k - 1].at[:, cols]
                    dst = wbuf.at[buf, side, pl.ds((member ^ k) * 256, 256), :]
                    pltpu.make_async_copy(src, dst, sem.at[buf]).start()

        @pl.when(jnp.logical_not(active))
        def _():
            for side in range(2):
                cols = pl.ds(side * FF + tile * i, tile)
                pltpu.make_async_copy(slot.at[0, :, cols], wbuf.at[buf, side], sem.at[buf]).start()

    fetch(0)
    for i in range(3):
        if i < 2:
            fetch(i + 1)
        pltpu.make_async_copy(wbuf.at[i % 2], wbuf.at[i % 2], sem.at[i % 2]).wait()
        gate = nn_dot(x[...], wbuf[i % 2, 0])
        up = nn_dot(x[...], wbuf[i % 2, 1])
        hidden = gate / (1.0 + jnp.exp(-gate)) * up
        out[:, tile * i : tile * (i + 1)] = hidden.astype(BF16)


def down_kernel(info, h, own, *refs):
    got = refs[0:7]
    slot, out, wbuf, sem = refs[7:]
    member = info[8]
    active = member < ACTIVE

    @pl.when(active)
    def _():
        for k in range(8):
            src = own.at[info[0]] if k == 0 else got[k - 1]
            pltpu.make_async_copy(src, wbuf.at[pl.ds((member ^ k) * 96, 96), :], sem.at[0]).start()

    @pl.when(jnp.logical_not(active))
    def _():
        pltpu.make_async_copy(slot.at[0], wbuf, sem.at[0]).start()

    row = iota((128, 96), 0)
    col = iota((128, 96), 1)
    owner = row >> 3
    place = row & 7
    main = ((place < CAP) & (col == 6 * owner + place)).astype(F32).astype(BF16)
    extra = []
    for j in range(3):
        hit = (place == 6) & (col == 6 * owner + j) | (place == 7) & (col == 6 * owner + 3 + j)
        extra.append(hit.astype(F32).astype(BF16))
    pltpu.make_async_copy(wbuf, wbuf, sem.at[0]).wait()
    last = nn_dot(h[...], wbuf[:, WIDE:]).astype(BF16)
    for j in range(3):
        y = nn_dot(h[...], wbuf[:, PART * j : PART * (j + 1)]).astype(BF16)
        for b in range(8):
            rows = slice(96 * b, 96 * (b + 1))
            packed = nn_dot(main, y[rows]) + nn_dot(extra[j], last[rows])
            out[128 * b : 128 * (b + 1), PART * j : PART * (j + 1)] = packed.astype(BF16)


def combine_kernel(route, gate, y, out):
    rank, gates = ranks(route[...], gate[...])
    high = gates.astype(BF16)
    low = (gates - high.astype(F32)).astype(BF16)
    every = spread()
    wide = nt_dot(rank.astype(BF16), every)
    high = nt_dot(high, every)
    low = nt_dot(low, every)
    place = (iota((TOK, ROWS), 1) & 7).astype(F32)
    main = (wide == place) & (place < CAP)
    tail = jnp.zeros((TOK, PART), F32)
    for j in range(3):
        wanted = jnp.where(place == 6, float(j), jnp.where(place == 7, float(3 + j), -2.0))
        ext = wide == wanted
        parts = [jnp.where(mask, g, 0.0) for mask in (main, ext) for g in (high, low)]
        stack = jnp.concatenate(parts, axis=0).astype(BF16)
        got = nn_dot(stack, y[:, PART * j : PART * (j + 1)])
        out[:, PART * j : PART * (j + 1)] = (got[0:TOK] + got[TOK : 2 * TOK]).astype(BF16)
        tail = tail + (got[2 * TOK : 3 * TOK] + got[3 * TOK :])
    out[:, WIDE:] = tail.astype(BF16)


def shape(*dims, dtype=BF16):
    return jax.ShapeDtypeStruct(dims, dtype)


def per_device(
    tokens,
    slot_route,
    route_gate,
    placement_table,
    refreshed,
    slot_gate_up,
    slot_down,
    new_gate_up,
    new_down,
):
    group = lax.axis_index("ep").astype(jnp.int32)
    member = lax.axis_index("dp").astype(jnp.int32)
    others = member ^ jnp.arange(MEMBERS, dtype=jnp.int32)
    slots = (((group - shift_of(others)) & 15) << 3) | others
    second = lax.dynamic_slice_in_dim(refreshed, 2 * group + 1, 1)
    picks = (placement_table[slots] == second).astype(jnp.int32)
    info = jnp.concatenate([picks, member[None]])

    staged = pl.pallas_call(
        stage_kernel,
        out_shape=[shape(256, WIDE)] * 7 + [shape(96, D)] * 7,
        in_specs=[SMEM, ANY, ANY],
        out_specs=[ANY] * 14,
        scratch_shapes=[
            pltpu.VMEM((2, 256, WIDE), BF16),
            pltpu.VMEM((2, 96, D), BF16),
            pltpu.SemaphoreType.DMA((2,)),
            pltpu.SemaphoreType.DMA((14,)),
        ],
        compiler_params=params(),
        name="stage",
    )(info, new_gate_up, new_down)

    def move(x, k):
        return lax.ppermute(x, "dp", [(d ^ k, d) for d in range(ACTIVE)])

    got_up = [move(staged[k - 1], k) for k in range(1, 8)]
    got_down = [move(staged[k + 6], k) for k in range(1, 8)]

    outgoing = pl.pallas_call(
        dispatch_kernel,
        out_shape=shape(ROWS, WIDE),
        in_specs=[VMEM, VMEM],
        out_specs=VMEM,
        compiler_params=params(),
        name="dispatch",
    )(slot_route, tokens)
    incoming = lax.all_to_all(
        outgoing.reshape(SLOTS, PACK, WIDE), ("ep", "dp"), split_axis=0, concat_axis=0, tiled=True
    ).reshape(ROWS, WIDE)
    rows = pl.pallas_call(
        compact_kernel,
        out_shape=shape(DENSE, D),
        in_specs=[VMEM],
        out_specs=VMEM,
        compiler_params=params(),
        name="compact",
    )(incoming)
    hidden = pl.pallas_call(
        up_kernel,
        out_shape=shape(DENSE, FF),
        in_specs=[SMEM, VMEM] + [ANY] * 9,
        out_specs=VMEM,
        scratch_shapes=[pltpu.VMEM((2, 2, D, 256), BF16), pltpu.SemaphoreType.DMA((2,))],
        compiler_params=params(),
        name="up",
    )(info, rows, new_gate_up, *got_up, slot_gate_up)
    results = pl.pallas_call(
        down_kernel,
        out_shape=shape(ROWS, WIDE),
        in_specs=[SMEM, VMEM] + [ANY] * 9,
        out_specs=VMEM,
        scratch_shapes=[pltpu.VMEM((FF, D), BF16), pltpu.SemaphoreType.DMA((1,))],
        compiler_params=params(),
        name="down",
    )(info, hidden, new_down, *got_down, slot_down)
    returned = lax.all_to_all(
        results.reshape(SLOTS, PACK, WIDE), ("ep", "dp"), split_axis=0, concat_axis=0, tiled=True
    ).reshape(ROWS, WIDE)
    return pl.pallas_call(
        combine_kernel,
        out_shape=shape(TOK, D),
        in_specs=[VMEM, VMEM, VMEM],
        out_specs=VMEM,
        compiler_params=params(),
        name="combine",
    )(slot_route, route_gate, returned)


def solution(mesh):
    return jax.shard_map(
        per_device,
        mesh=mesh,
        in_specs=(
            P(("ep", "dp"), None),
            P(("ep", "dp"), None),
            P(("ep", "dp"), None),
            P(),
            P(),
            P(("ep", "dp"), None, None),
            P(("ep", "dp"), None, None),
            P("ep", "dp", None),
            P("ep", "dp", None),
        ),
        out_specs=P(("ep", "dp"), None),
        check_vma=False,
    )
```

```python
import jax
import jax.numpy as jnp
from jax import lax
from jax.experimental import pallas as pl
from jax.experimental.pallas import tpu as pltpu
from jax.sharding import PartitionSpec as P


D = 2048
FF = 768
TOP = 8
CAP = 6
TOK = 64
SLOTS = 128
MEMBERS = 8
ACTIVE = 6
PACK = 8
WIDE = 1536
PART = 512
ROWS = SLOTS * PACK
DENSE = SLOTS * CAP


ANY = pl.BlockSpec(memory_space=pl.ANY)
SMEM = pl.BlockSpec(memory_space=pltpu.SMEM)
VMEM = pl.BlockSpec(memory_space=pltpu.VMEM)
F32 = jnp.float32
BF16 = jnp.bfloat16


def params():
    return pltpu.CompilerParams(vmem_limit_bytes=56 * 1024 * 1024)


def iota(shape, dim):
    return lax.broadcasted_iota(jnp.int32, shape, dim)


def nt_dot(a, b):
    return lax.dot_general(a, b, (((1,), (1,)), ((), ())), preferred_element_type=F32)


def nn_dot(a, b):
    return jnp.dot(a, b, preferred_element_type=F32)


def shift_of(member):
    return jnp.where(member < 4, member, jnp.where(member == 4, 8, jnp.where(member == 5, 15, 0)))


def home_of(slot):
    member = slot & 7
    return ((((slot >> 3) + shift_of(member)) & 15) << 3) | member


def pick_of(ids, table, refreshed, other):
    group = ids[0]
    slot = (((group - shift_of(other)) & 15) << 3) | other
    return (table[slot] == refreshed[2 * group + 1]).astype(jnp.int32)


def hits_of(home, k):
    return iota((SLOTS, TOK), 0) == home[k : k + 1, :]


def ranks(home):
    hits = jnp.zeros((SLOTS, TOK), F32)
    for k in range(TOP):
        hits = jnp.where(hits_of(home, k), 1.0, hits)
    before = (iota((TOK, TOK), 0) < iota((TOK, TOK), 1)).astype(F32).astype(BF16)
    rank = nn_dot(hits.astype(BF16), before)
    return jnp.where(hits > 0, rank, -1.0).astype(BF16)


def spread():
    return ((iota((ROWS, SLOTS), 0) >> 3) == iota((ROWS, SLOTS), 1)).astype(F32).astype(BF16)


def stage_kernel(ids, table, refreshed, gu, *refs):
    outs, (vgu, sem_in, sem_out) = refs[0:7], refs[7:]
    load = pltpu.make_async_copy(gu, vgu, sem_in.at[0])
    load.start()
    picks = [pick_of(ids, table, refreshed, ids[1] ^ k) for k in range(1, 8)]
    load.wait()
    copies = []
    for k in range(7):
        copies.append(pltpu.make_async_copy(vgu.at[picks[k]], outs[k], sem_out.at[k]))
        copies[-1].start()
    for c in copies:
        c.wait()


def relay_kernel(ids, table, refreshed, own, swapped, *refs):
    outs, (vown, vswap, sem_in, sem_out) = refs[0:3], refs[3:]
    loads = [
        pltpu.make_async_copy(own, vown, sem_in.at[0]),
        pltpu.make_async_copy(swapped, vswap, sem_in.at[1]),
    ]
    for c in loads:
        c.start()
    picks = [pick_of(ids, table, refreshed, ids[1] ^ k) for k in range(1, 4)]
    for c in loads:
        c.wait()
    copies = []
    for k in range(3):
        for n, src in enumerate((vown, vswap)):
            copies.append(pltpu.make_async_copy(src.at[picks[k]], outs[k].at[n], sem_out.at[2 * k + n]))
            copies[-1].start()
    for c in copies:
        c.wait()


def dispatch_kernel(route, tokens, out):
    rank = ranks(home_of(route[...]))
    twice = jnp.concatenate([rank, rank], axis=1)
    wide = nn_dot(spread(), twice)
    place = (iota((ROWS, SLOTS), 0) & 7).astype(F32)
    left = iota((ROWS, SLOTS), 1) < TOK
    main = left & (wide == place) & (place < CAP)
    for j in range(3):
        wanted = jnp.where(place == 6, float(j), jnp.where(place == 7, float(3 + j), -2.0))
        pick = (main | (jnp.logical_not(left) & (wide == wanted))).astype(F32).astype(BF16)
        rhs = jnp.concatenate([tokens[:, PART * j : PART * (j + 1)], tokens[:, WIDE:]], axis=0)
        out[:, PART * j : PART * (j + 1)] = nn_dot(pick, rhs).astype(BF16)


def compact_kernel(x, out):
    row = iota((96, 128), 0)
    col = iota((96, 128), 1)
    owner = row // 6
    rank = row - 6 * owner
    main = (col == 8 * owner + rank).astype(F32).astype(BF16)
    extra = []
    for j in range(3):
        hit = (col == 8 * owner + 6) & (rank == j) | (col == 8 * owner + 7) & (rank == 3 + j)
        extra.append(hit.astype(F32).astype(BF16))
    extra = jnp.concatenate(extra, axis=1)
    for b in range(8):
        blk = x[128 * b : 128 * (b + 1), :]
        out[96 * b : 96 * (b + 1), 0:WIDE] = nn_dot(main, blk).astype(BF16)
        tall = jnp.concatenate([blk[:, PART * j : PART * (j + 1)] for j in range(3)], axis=0)
        out[96 * b : 96 * (b + 1), WIDE:] = nn_dot(extra, tall).astype(BF16)


def up_kernel(ids, table, refreshed, x, own, *refs):
    got = refs[0:7]
    slot, out, wbuf, sem = refs[7:]
    member = ids[1]
    active = member < ACTIVE
    pick = pick_of(ids, table, refreshed, member)
    tile = 256

    def fetch(i):
        buf = i % 2

        @pl.when(active)
        def _():
            for side in range(2):
                cols = pl.ds(side * FF + tile * i, tile)
                for k in range(8):
                    src = own.at[pick, :, cols] if k == 0 else got[k - 1].at[:, cols]
                    dst = wbuf.at[buf, side, pl.ds((member ^ k) * 256, 256), :]
                    pltpu.make_async_copy(src, dst, sem.at[buf]).start()

        @pl.when(jnp.logical_not(active))
        def _():
            for side in range(2):
                cols = pl.ds(side * FF + tile * i, tile)
                pltpu.make_async_copy(slot.at[0, :, cols], wbuf.at[buf, side], sem.at[buf]).start()

    fetch(0)
    for i in range(3):
        if i < 2:
            fetch(i + 1)
        pltpu.make_async_copy(wbuf.at[i % 2], wbuf.at[i % 2], sem.at[i % 2]).wait()
        gate = nn_dot(x[...], wbuf[i % 2, 0])
        up = nn_dot(x[...], wbuf[i % 2, 1])
        hidden = gate / (1.0 + jnp.exp(-gate)) * up
        out[:, tile * i : tile * (i + 1)] = hidden.astype(BF16)


def down_kernel(ids, table, refreshed, h, own, swapped, *refs):
    got = refs[0:3]
    slot, out, wbuf, sem = refs[3:]
    member = ids[1]
    active = member < ACTIVE
    pick = pick_of(ids, table, refreshed, member)

    @pl.when(active)
    def _():
        for k in range(4):
            for n in range(2):
                if k == 0:
                    src = (own, swapped)[n].at[pick]
                else:
                    src = got[k - 1].at[n]
                dst = wbuf.at[pl.ds((member ^ (k + 4 * n)) * 96, 96), :]
                pltpu.make_async_copy(src, dst, sem.at[0]).start()

    @pl.when(jnp.logical_not(active))
    def _():
        pltpu.make_async_copy(slot.at[0], wbuf, sem.at[0]).start()

    row = iota((128, 96), 0)
    col = iota((128, 96), 1)
    owner = row >> 3
    place = row & 7
    main = ((place < CAP) & (col == 6 * owner + place)).astype(F32).astype(BF16)
    extra = []
    for j in range(3):
        hit = (place == 6) & (col == 6 * owner + j) | (place == 7) & (col == 6 * owner + 3 + j)
        extra.append(hit.astype(F32).astype(BF16))
    pltpu.make_async_copy(wbuf, wbuf, sem.at[0]).wait()
    last = nn_dot(h[...], wbuf[:, WIDE:]).astype(BF16)
    for j in range(3):
        y = nn_dot(h[...], wbuf[:, PART * j : PART * (j + 1)]).astype(BF16)
        for b in range(8):
            rows = slice(96 * b, 96 * (b + 1))
            packed = nn_dot(main, y[rows]) + nn_dot(extra[j], last[rows])
            out[128 * b : 128 * (b + 1), PART * j : PART * (j + 1)] = packed.astype(BF16)


def weigh_kernel(route, gate, out):
    home = home_of(route[...])
    gates = jnp.zeros((SLOTS, TOK), F32)
    for k in range(TOP):
        gates = jnp.where(hits_of(home, k), gate[k : k + 1, :], gates)
    high = gates.astype(BF16)
    low = (gates - high.astype(F32)).astype(BF16)
    eye = (iota((TOK, TOK), 0) == iota((TOK, TOK), 1)).astype(F32).astype(BF16)
    every = spread()
    wide, high, low = [
        nt_dot(nt_dot(eye, v).astype(BF16), every) for v in (ranks(home), high, low)
    ]
    place = (iota((TOK, ROWS), 1) & 7).astype(F32)
    masks = [(wide == place) & (place < CAP)]
    for j in range(3):
        wanted = jnp.where(place == 6, float(j), jnp.where(place == 7, float(3 + j), -2.0))
        masks.append(wide == wanted)
    for i, mask in enumerate(masks):
        out[i, 0:TOK, :] = jnp.where(mask, high, 0.0).astype(BF16)
        out[i, TOK:, :] = jnp.where(mask, low, 0.0).astype(BF16)


def combine_kernel(weight, y, out):
    tail = jnp.zeros((TOK, PART), F32)
    for j in range(3):
        part = y[:, PART * j : PART * (j + 1)]
        stack = jnp.concatenate([weight[0], weight[1 + j]], axis=0)
        got = nn_dot(stack, part)
        out[:, PART * j : PART * (j + 1)] = (got[0:TOK] + got[TOK : 2 * TOK]).astype(BF16)
        tail = tail + (got[2 * TOK : 3 * TOK] + got[3 * TOK :])
    out[:, WIDE:] = tail.astype(BF16)


def resident(x):
    return pltpu.with_memory_space_constraint(x, pltpu.VMEM)


def shape(*dims, dtype=BF16):
    return jax.ShapeDtypeStruct(dims, dtype)


def per_device(
    tokens,
    slot_route,
    route_gate,
    placement_table,
    refreshed,
    slot_gate_up,
    slot_down,
    new_gate_up,
    new_down,
):
    ids = jnp.stack([lax.axis_index("ep"), lax.axis_index("dp")]).astype(jnp.int32)
    where = (ids, placement_table, refreshed)
    route = slot_route.T
    gate = route_gate.T

    swapped = lax.ppermute(new_down, "dp", [(d ^ 4, d) for d in range(MEMBERS)])
    staged = pl.pallas_call(
        stage_kernel,
        out_shape=[shape(256, WIDE)] * 7,
        in_specs=[SMEM] * 3 + [ANY],
        out_specs=[ANY] * 7,
        scratch_shapes=[
            pltpu.VMEM((2, 256, WIDE), BF16),
            pltpu.SemaphoreType.DMA((1,)),
            pltpu.SemaphoreType.DMA((7,)),
        ],
        compiler_params=params(),
        name="stage",
    )(*where, new_gate_up)

    def move(x, k):
        return lax.ppermute(x, "dp", [(d ^ k, d) for d in range(ACTIVE)])

    got_up = []
    for k in range(1, 8):
        got_up.append(move(staged[k - 1], k))

    outgoing = pl.pallas_call(
        dispatch_kernel,
        out_shape=shape(ROWS, WIDE),
        in_specs=[VMEM, VMEM],
        out_specs=VMEM,
        compiler_params=params(),
        name="dispatch",
    )(route, tokens)
    incoming = lax.all_to_all(
        outgoing.reshape(SLOTS, PACK, WIDE), ("ep", "dp"), split_axis=0, concat_axis=0, tiled=True
    )
    incoming = resident(incoming.reshape(ROWS, WIDE))
    relayed = pl.pallas_call(
        relay_kernel,
        out_shape=[shape(2, 96, D)] * 3,
        in_specs=[SMEM] * 3 + [ANY] * 2,
        out_specs=[ANY] * 3,
        scratch_shapes=[
            pltpu.VMEM((2, 96, D), BF16),
            pltpu.VMEM((2, 96, D), BF16),
            pltpu.SemaphoreType.DMA((2,)),
            pltpu.SemaphoreType.DMA((6,)),
        ],
        compiler_params=params(),
        name="relay",
    )(*where, new_down, swapped)
    got_down = []
    for k in range(1, 4):
        got_down.append(move(relayed[k - 1], k))
    weight = pl.pallas_call(
        weigh_kernel,
        out_shape=shape(4, 2 * TOK, ROWS),
        in_specs=[VMEM, VMEM],
        out_specs=VMEM,
        compiler_params=params(),
        name="weigh",
    )(route, gate)
    rows = pl.pallas_call(
        compact_kernel,
        out_shape=shape(DENSE, D),
        in_specs=[VMEM],
        out_specs=VMEM,
        compiler_params=params(),
        name="compact",
    )(incoming)
    hidden = pl.pallas_call(
        up_kernel,
        out_shape=shape(DENSE, FF),
        in_specs=[SMEM] * 3 + [VMEM] + [ANY] * 9,
        out_specs=VMEM,
        scratch_shapes=[pltpu.VMEM((2, 2, D, 256), BF16), pltpu.SemaphoreType.DMA((2,))],
        compiler_params=params(),
        name="up",
    )(*where, rows, new_gate_up, *got_up, slot_gate_up)
    results = pl.pallas_call(
        down_kernel,
        out_shape=shape(ROWS, WIDE),
        in_specs=[SMEM] * 3 + [VMEM] + [ANY] * 6,
        out_specs=VMEM,
        scratch_shapes=[pltpu.VMEM((FF, D), BF16), pltpu.SemaphoreType.DMA((1,))],
        compiler_params=params(),
        name="down",
    )(*where, hidden, new_down, swapped, *got_down, slot_down)
    returned = lax.all_to_all(
        results.reshape(SLOTS, PACK, WIDE), ("ep", "dp"), split_axis=0, concat_axis=0, tiled=True
    )
    returned = resident(returned.reshape(ROWS, WIDE))
    return pl.pallas_call(
        combine_kernel,
        out_shape=shape(TOK, D),
        in_specs=[VMEM, VMEM],
        out_specs=VMEM,
        compiler_params=params(),
        name="combine",
    )(weight, returned)


def solution(mesh):
    return jax.shard_map(
        per_device,
        mesh=mesh,
        in_specs=(
            P(("ep", "dp"), None),
            P(("ep", "dp"), None),
            P(("ep", "dp"), None),
            P(),
            P(),
            P(("ep", "dp"), None, None),
            P(("ep", "dp"), None, None),
            P("ep", "dp", None),
            P("ep", "dp", None),
        ),
        out_specs=P(("ep", "dp"), None),
        check_vma=False,
    )
```

```python
import jax
import jax.numpy as jnp
from jax import lax
from jax.experimental import pallas as pl
from jax.experimental.pallas import tpu as pltpu
from jax.sharding import Mesh
from jax.sharding import PartitionSpec as P


D = 2048
FF = 768
TOP = 8
CAP = 6
TOK = 64
SLOTS = 128
ACTIVE = 6
PACK = 8
WIDE = 1536
PART = 512
EP = ("y", "zh", "core")
DP = ("zl", "x")
EVERY = EP + DP
COLUMN = EP + ("zl",)
ROWS = SLOTS * PACK
DENSE = SLOTS * CAP


ANY = pl.BlockSpec(memory_space=pl.ANY)
SMEM = pl.BlockSpec(memory_space=pltpu.SMEM)
VMEM = pl.BlockSpec(memory_space=pltpu.VMEM)
F32 = jnp.float32
BF16 = jnp.bfloat16


def params():
    return pltpu.CompilerParams(vmem_limit_bytes=56 * 1024 * 1024)


def iota(shape, dim):
    return lax.broadcasted_iota(jnp.int32, shape, dim)


def nt_dot(a, b):
    return lax.dot_general(a, b, (((1,), (1,)), ((), ())), preferred_element_type=F32)


def nn_dot(a, b):
    return jnp.dot(a, b, preferred_element_type=F32)


def shift_of(member):
    return jnp.where(member < 4, member, jnp.where(member == 4, 8, jnp.where(member == 5, 15, 0)))


def home_of(slot):
    member = slot & 7
    return ((((slot >> 3) + shift_of(member)) & 15) << 3) | member


def pick_of(ids, table, refreshed, other):
    group = ids[0]
    slot = (((group - shift_of(other)) & 15) << 3) | other
    return (table[slot] == refreshed[2 * group + 1]).astype(jnp.int32)


def hits_of(home, k):
    return iota((SLOTS, TOK), 0) == home[k : k + 1, :]


def ranks(home):
    hits = jnp.zeros((SLOTS, TOK), F32)
    for k in range(TOP):
        hits = jnp.where(hits_of(home, k), 1.0, hits)
    before = (iota((TOK, TOK), 0) < iota((TOK, TOK), 1)).astype(F32).astype(BF16)
    rank = nn_dot(hits.astype(BF16), before)
    return jnp.where(hits > 0, rank, -1.0).astype(BF16)


def spread():
    return ((iota((ROWS, SLOTS), 0) >> 3) == iota((ROWS, SLOTS), 1)).astype(F32).astype(BF16)


def copy_all(pairs, sems):
    copies = [pltpu.make_async_copy(src, dst, sems.at[n]) for n, (src, dst) in enumerate(pairs)]
    for c in copies:
        c.start()
    for c in copies:
        c.wait()


def stage_kernel(ids, table, refreshed, *refs):
    count = (len(refs) - 5) // 2
    sources, outs, sem_in, sem_out = refs[:count], refs[count : count + 3], refs[-2], refs[-1]
    held = refs[count + 3 : -2]
    picks = [pick_of(ids, table, refreshed, ids[1] ^ k) for k in range(1, 4)]
    copy_all(list(zip(sources, held)), sem_in)
    copy_all(
        [
            (held[n].at[picks[k]], outs[k].at[n] if count > 1 else outs[k])
            for k in range(3)
            for n in range(count)
        ],
        sem_out,
    )


def dispatch_kernel(ids, *refs):
    packed, out = refs[:4], refs[4]
    column = ids[1] & 3
    lanes = iota((TOK, SLOTS), 1)
    lower = (iota((TOK, TOK), 0) > iota((TOK, TOK), 1)).astype(F32).astype(BF16)
    part = 32 * PACK
    every = (iota((part, SLOTS), 1) == 4 * (iota((part, SLOTS), 0) >> 3) + column).astype(F32)
    every = every.astype(BF16)
    place = (iota((part, SLOTS), 0) & 7).astype(F32)
    left = iota((part, SLOTS), 1) < TOK
    for k in range(4):
        home = home_of(packed[k][:, D:].astype(F32).astype(jnp.int32))
        hits = jnp.zeros((TOK, SLOTS), F32)
        for n in range(TOP):
            hits = jnp.where(home[:, n : n + 1] == lanes, 1.0, hits)
        rank = jnp.where(hits > 0, nn_dot(lower, hits.astype(BF16)), -1.0).astype(BF16)
        wide = nt_dot(every, jnp.concatenate([rank, rank], axis=0))
        main = left & (wide == place) & (place < CAP)
        for j in range(3):
            wanted = jnp.where(place == 6, float(j), jnp.where(place == 7, float(3 + j), -2.0))
            pick = (main | (jnp.logical_not(left) & (wide == wanted))).astype(F32).astype(BF16)
            cols = slice(PART * j, PART * (j + 1))
            rhs = jnp.concatenate([packed[k][:, cols], packed[k][:, WIDE:D]], axis=0)
            got = nn_dot(pick, rhs).reshape(32, PACK, PART)
            out[:, column ^ k, :, cols] = got.astype(BF16)


def compact_kernel(x, out):
    row = iota((96, 128), 0)
    col = iota((96, 128), 1)
    owner = row // 6
    rank = row - 6 * owner
    main = (col == 8 * owner + rank).astype(F32).astype(BF16)
    extra = []
    for j in range(3):
        hit = (col == 8 * owner + 6) & (rank == j) | (col == 8 * owner + 7) & (rank == 3 + j)
        extra.append(hit.astype(F32).astype(BF16))
    extra = jnp.concatenate(extra, axis=1)
    for b in range(8):
        blk = x[128 * b : 128 * (b + 1), :]
        out[96 * b : 96 * (b + 1), 0:WIDE] = nn_dot(main, blk).astype(BF16)
        tall = jnp.concatenate([blk[:, PART * j : PART * (j + 1)] for j in range(3)], axis=0)
        out[96 * b : 96 * (b + 1), WIDE:] = nn_dot(extra, tall).astype(BF16)


def up_kernel(ids, table, refreshed, x, own, swapped, *refs):
    got = refs[0:6]
    slot, out, wbuf, sem = refs[6:]
    member = ids[1]
    active = member < ACTIVE
    pick = pick_of(ids, table, refreshed, member)
    tile = 256

    def fetch(i):
        buf = i % 2

        @pl.when(active)
        def _():
            for side in range(2):
                cols = pl.ds(side * FF + tile * i, tile)
                for k in range(4):
                    for n in range(2):
                        if k == 0:
                            src = (own, swapped)[n].at[pick, :, cols]
                        else:
                            src = got[3 * n + k - 1].at[:, cols]
                        dst = wbuf.at[buf, side, pl.ds((member ^ (k + 4 * n)) * 256, 256), :]
                        pltpu.make_async_copy(src, dst, sem.at[buf]).start()

        @pl.when(jnp.logical_not(active))
        def _():
            for side in range(2):
                cols = pl.ds(side * FF + tile * i, tile)
                pltpu.make_async_copy(slot.at[0, :, cols], wbuf.at[buf, side], sem.at[buf]).start()

    fetch(0)
    for i in range(3):
        if i < 2:
            fetch(i + 1)
        pltpu.make_async_copy(wbuf.at[i % 2], wbuf.at[i % 2], sem.at[i % 2]).wait()
        gate = nn_dot(x[...], wbuf[i % 2, 0])
        up = nn_dot(x[...], wbuf[i % 2, 1])
        hidden = gate / (1.0 + jnp.exp(-gate)) * up
        out[:, tile * i : tile * (i + 1)] = hidden.astype(BF16)


def down_kernel(ids, table, refreshed, h, own, swapped, *refs):
    got = refs[0:3]
    slot, out, wbuf, sem = refs[3:]
    member = ids[1]
    active = member < ACTIVE
    pick = pick_of(ids, table, refreshed, member)

    @pl.when(active)
    def _():
        for k in range(4):
            for n in range(2):
                if k == 0:
                    src = (own, swapped)[n].at[pick]
                else:
                    src = got[k - 1].at[n]
                dst = wbuf.at[pl.ds((member ^ (k + 4 * n)) * 96, 96), :]
                pltpu.make_async_copy(src, dst, sem.at[0]).start()

    @pl.when(jnp.logical_not(active))
    def _():
        pltpu.make_async_copy(slot.at[0], wbuf, sem.at[0]).start()

    row = iota((128, 96), 0)
    col = iota((128, 96), 1)
    owner = row >> 3
    place = row & 7
    main = ((place < CAP) & (col == 6 * owner + place)).astype(F32).astype(BF16)
    extra = []
    for j in range(3):
        hit = (place == 6) & (col == 6 * owner + j) | (place == 7) & (col == 6 * owner + 3 + j)
        extra.append(hit.astype(F32).astype(BF16))
    pltpu.make_async_copy(wbuf, wbuf, sem.at[0]).wait()
    last = nn_dot(h[...], wbuf[:, WIDE:]).astype(BF16)
    for j in range(3):
        y = nn_dot(h[...], wbuf[:, PART * j : PART * (j + 1)]).astype(BF16)
        for b in range(8):
            rows = slice(96 * b, 96 * (b + 1))
            packed = nn_dot(main, y[rows]) + nn_dot(extra[j], last[rows])
            out[128 * b : 128 * (b + 1), PART * j : PART * (j + 1)] = packed.astype(BF16)


def weigh_kernel(route, gate, out):
    home = home_of(route[...])
    gates = jnp.zeros((SLOTS, TOK), F32)
    for k in range(TOP):
        gates = jnp.where(hits_of(home, k), gate[k : k + 1, :], gates)
    high = gates.astype(BF16)
    low = (gates - high.astype(F32)).astype(BF16)
    eye = (iota((TOK, TOK), 0) == iota((TOK, TOK), 1)).astype(F32).astype(BF16)
    every = spread()
    wide, high, low = [
        nt_dot(nt_dot(eye, v).astype(BF16), every) for v in (ranks(home), high, low)
    ]
    place = (iota((TOK, ROWS), 1) & 7).astype(F32)
    masks = [(wide == place) & (place < CAP)]
    for j in range(3):
        wanted = jnp.where(place == 6, float(j), jnp.where(place == 7, float(3 + j), -2.0))
        masks.append(wide == wanted)
    for i, mask in enumerate(masks):
        out[i, 0:TOK, :] = jnp.where(mask, high, 0.0).astype(BF16)
        out[i, TOK:, :] = jnp.where(mask, low, 0.0).astype(BF16)


def combine_kernel(weight, y, out):
    tail = jnp.zeros((TOK, PART), F32)
    for j in range(3):
        part = y[:, PART * j : PART * (j + 1)]
        stack = jnp.concatenate([weight[0], weight[1 + j]], axis=0)
        got = nn_dot(stack, part)
        out[:, PART * j : PART * (j + 1)] = (got[0:TOK] + got[TOK : 2 * TOK]).astype(BF16)
        tail = tail + (got[2 * TOK : 3 * TOK] + got[3 * TOK :])
    out[:, WIDE:] = tail.astype(BF16)


def resident(x):
    return pltpu.with_memory_space_constraint(x, pltpu.VMEM)


def shape(*dims, dtype=BF16):
    return jax.ShapeDtypeStruct(dims, dtype)


def per_device(
    tokens,
    slot_route,
    route_gate,
    placement_table,
    refreshed,
    slot_gate_up,
    slot_down,
    new_gate_up,
    new_down,
):
    ids = jnp.stack([lax.axis_index(EP), lax.axis_index(DP)]).astype(jnp.int32)
    where = (ids, placement_table, refreshed)
    route = slot_route.T
    gate = route_gate.T

    def swap(x):
        return lax.ppermute(x, "zl", [(0, 1), (1, 0)])

    def move(x, k):
        return lax.ppermute(x, DP, [(d ^ k, d) for d in range(ACTIVE)])

    def stage(dims, *sources):
        count = len(sources)
        held = [2] * (count > 1) + list(dims)
        return pl.pallas_call(
            stage_kernel,
            out_shape=[shape(*held)] * 3,
            in_specs=[SMEM] * 3 + [ANY] * count,
            out_specs=[ANY] * 3,
            scratch_shapes=[pltpu.VMEM((2, *dims), BF16)] * count
            + [pltpu.SemaphoreType.DMA((count,)), pltpu.SemaphoreType.DMA((3 * count,))],
            compiler_params=params(),
        )(*where, *sources)

    swapped_up = swap(new_gate_up)
    swapped_down = swap(new_down)
    marks = jnp.pad(slot_route.astype(BF16), ((0, 0), (0, 120)))
    packed = [jnp.concatenate([tokens, marks], axis=1)]
    for k in range(1, 4):
        packed.append(lax.ppermute(packed[0], "x", [(d ^ k, d) for d in range(4)]))
    own = stage((256, WIDE), new_gate_up)
    got_up = []
    for k in range(1, 4):
        got_up.append(move(own[k - 1], k))
    outgoing = pl.pallas_call(
        dispatch_kernel,
        out_shape=shape(32, 4, PACK, WIDE),
        in_specs=[SMEM] + [VMEM] * 4,
        out_specs=VMEM,
        compiler_params=params(),
        name="dispatch",
    )(ids, *[resident(p) for p in packed])
    incoming = lax.all_to_all(
        outgoing.reshape(32, 4 * PACK, WIDE), COLUMN, split_axis=0, concat_axis=0, tiled=True
    )
    incoming = resident(incoming.reshape(ROWS, WIDE))
    far = stage((256, WIDE), swapped_up)
    for k in range(1, 4):
        got_up.append(move(far[k - 1], k))
    both = stage((96, D), new_down, swapped_down)
    got_down = []
    for k in range(1, 4):
        got_down.append(move(both[k - 1], k))
    weight = pl.pallas_call(
        weigh_kernel,
        out_shape=shape(4, 2 * TOK, ROWS),
        in_specs=[VMEM, VMEM],
        out_specs=VMEM,
        compiler_params=params(),
        name="weigh",
    )(route, gate)
    rows = pl.pallas_call(
        compact_kernel,
        out_shape=shape(DENSE, D),
        in_specs=[VMEM],
        out_specs=VMEM,
        compiler_params=params(),
        name="compact",
    )(incoming)
    hidden = pl.pallas_call(
        up_kernel,
        out_shape=shape(DENSE, FF),
        in_specs=[SMEM] * 3 + [VMEM] + [ANY] * 9,
        out_specs=VMEM,
        scratch_shapes=[pltpu.VMEM((2, 2, D, 256), BF16), pltpu.SemaphoreType.DMA((2,))],
        compiler_params=params(),
        name="up",
    )(*where, rows, new_gate_up, swapped_up, *got_up, slot_gate_up)
    results = pl.pallas_call(
        down_kernel,
        out_shape=shape(ROWS, WIDE),
        in_specs=[SMEM] * 3 + [VMEM] + [ANY] * 6,
        out_specs=VMEM,
        scratch_shapes=[pltpu.VMEM((FF, D), BF16), pltpu.SemaphoreType.DMA((1,))],
        compiler_params=params(),
        name="down",
    )(*where, hidden, new_down, swapped_down, *got_down, slot_down)
    returned = lax.all_to_all(
        results.reshape(SLOTS, PACK, WIDE), EVERY, split_axis=0, concat_axis=0, tiled=True
    )
    returned = resident(returned.reshape(ROWS, WIDE))
    return pl.pallas_call(
        combine_kernel,
        out_shape=shape(TOK, D),
        in_specs=[VMEM, VMEM],
        out_specs=VMEM,
        compiler_params=params(),
        name="combine",
    )(weight, returned)


def solution(mesh):
    split = Mesh(mesh.devices.reshape(4, 2, 2, 2, 4), EVERY)
    return jax.shard_map(
        per_device,
        mesh=split,
        in_specs=(
            P(EVERY, None),
            P(EVERY, None),
            P(EVERY, None),
            P(),
            P(),
            P(EVERY, None, None),
            P(EVERY, None, None),
            P(EP, DP, None),
            P(EP, DP, None),
        ),
        out_specs=P(EVERY, None),
        check_vma=False,
    )
```

```python
import jax
import jax.numpy as jnp
from jax import lax
from jax.experimental import pallas as pl
from jax.experimental.pallas import tpu as pltpu
from jax.sharding import Mesh
from jax.sharding import PartitionSpec as P


D = 2048
FF = 768
TOP = 8
CAP = 6
TOK = 64
SLOTS = 128
ACTIVE = 6
PACK = 8
WIDE = 1536
PART = 512
EP = ("y", "zh", "core")
DP = ("zl", "x")
EVERY = EP + DP
COLUMN = EP + ("zl",)
ROWS = SLOTS * PACK
DENSE = SLOTS * CAP


HBM = pl.BlockSpec(memory_space=pltpu.HBM)
SMEM = pl.BlockSpec(memory_space=pltpu.SMEM)
VMEM = pl.BlockSpec(memory_space=pltpu.VMEM)
F32 = jnp.float32
BF16 = jnp.bfloat16


def params(mib=20):
    return pltpu.CompilerParams(vmem_limit_bytes=mib * 1024 * 1024)


def iota(shape, dim):
    return lax.broadcasted_iota(jnp.int32, shape, dim)


def nt_dot(a, b):
    return lax.dot_general(a, b, (((1,), (1,)), ((), ())), preferred_element_type=F32)


def nn_dot(a, b):
    return jnp.dot(a, b, preferred_element_type=F32)


def shift_of(member):
    return jnp.where(member < 4, member, jnp.where(member == 4, 8, jnp.where(member == 5, 15, 0)))


def home_of(slot):
    member = slot & 7
    return ((((slot >> 3) + shift_of(member)) & 15) << 3) | member


def pick_of(ids, table, refreshed, other):
    group = ids[0]
    slot = (((group - shift_of(other)) & 15) << 3) | other
    return (table[slot] == refreshed[2 * group + 1]).astype(jnp.int32)


def hits_of(home, k):
    return iota((SLOTS, TOK), 0) == home[k : k + 1, :]


def ranks(home):
    hits = jnp.zeros((SLOTS, TOK), F32)
    for k in range(TOP):
        hits = jnp.where(hits_of(home, k), 1.0, hits)
    before = (iota((TOK, TOK), 0) < iota((TOK, TOK), 1)).astype(F32).astype(BF16)
    rank = nn_dot(hits.astype(BF16), before)
    return jnp.where(hits > 0, rank, -1.0).astype(BF16)


def spread():
    return ((iota((ROWS, SLOTS), 0) >> 3) == iota((ROWS, SLOTS), 1)).astype(F32).astype(BF16)


def copy_all(pairs, sems):
    copies = [pltpu.make_async_copy(src, dst, sems.at[n]) for n, (src, dst) in enumerate(pairs)]
    for c in copies:
        c.start()
    for c in copies:
        c.wait()


def stage_kernel(ids, table, refreshed, *refs):
    count = (len(refs) - 5) // 2
    sources, outs, sem_in, sem_out = refs[:count], refs[count : count + 3], refs[-2], refs[-1]
    held = refs[count + 3 : -2]
    picks = [pick_of(ids, table, refreshed, ids[1] ^ k) for k in range(1, 4)]
    copy_all(list(zip(sources, held)), sem_in)
    copy_all(
        [
            (held[n].at[picks[k]], outs[k].at[n] if count > 1 else outs[k])
            for k in range(3)
            for n in range(count)
        ],
        sem_out,
    )


def dispatch_kernel(ids, *refs):
    packed, out = refs[:4], refs[4]
    column = ids[1] & 3
    lanes = iota((TOK, SLOTS), 1)
    lower = (iota((TOK, TOK), 0) > iota((TOK, TOK), 1)).astype(F32).astype(BF16)
    part = 32 * PACK
    every = (iota((part, SLOTS), 1) == 4 * (iota((part, SLOTS), 0) >> 3) + column).astype(F32)
    every = every.astype(BF16)
    place = (iota((part, SLOTS), 0) & 7).astype(F32)
    left = iota((part, SLOTS), 1) < TOK
    for k in range(4):
        home = home_of(packed[k][:, D:].astype(F32).astype(jnp.int32))
        hits = jnp.zeros((TOK, SLOTS), F32)
        for n in range(TOP):
            hits = jnp.where(home[:, n : n + 1] == lanes, 1.0, hits)
        rank = jnp.where(hits > 0, nn_dot(lower, hits.astype(BF16)), -1.0).astype(BF16)
        wide = nt_dot(every, jnp.concatenate([rank, rank], axis=0))
        main = left & (wide == place) & (place < CAP)
        for j in range(3):
            wanted = jnp.where(place == 6, float(j), jnp.where(place == 7, float(3 + j), -2.0))
            pick = (main | (jnp.logical_not(left) & (wide == wanted))).astype(F32).astype(BF16)
            cols = slice(PART * j, PART * (j + 1))
            rhs = jnp.concatenate([packed[k][:, cols], packed[k][:, WIDE:D]], axis=0)
            got = nn_dot(pick, rhs).reshape(32, PACK, PART)
            out[:, column ^ k, :, cols] = got.astype(BF16)


def compact_kernel(x, out):
    row = iota((96, 128), 0)
    col = iota((96, 128), 1)
    rank = row >> 4
    base = (row & 15) * 8
    main = (col == base + rank).astype(F32).astype(BF16)
    extra = []
    for j in range(3):
        hit = (col == base + 6) & (rank == j) | (col == base + 7) & (rank == 3 + j)
        extra.append(hit.astype(F32).astype(BF16))
    extra = jnp.concatenate(extra, axis=1)
    for b in range(8):
        blk = x[128 * b : 128 * (b + 1), :]
        head = nn_dot(main, blk).astype(BF16)
        tall = jnp.concatenate([blk[:, PART * j : PART * (j + 1)] for j in range(3)], axis=0)
        tail = nn_dot(extra, tall).astype(BF16)
        for r in range(CAP):
            rows = slice(128 * r + 16 * b, 128 * r + 16 * (b + 1))
            out[rows, 0:WIDE] = head[16 * r : 16 * (r + 1)]
            out[rows, WIDE:] = tail[16 * r : 16 * (r + 1)]


def up_kernel(ids, table, refreshed, x, own, swapped, *refs):
    got = refs[0:6]
    slot, out, wbuf, sem = refs[6:]
    member = ids[1]
    active = member < ACTIVE
    pick = pick_of(ids, table, refreshed, member)
    tile = 256

    def fetch(i):
        buf = i % 2

        @pl.when(active)
        def _():
            for side in range(2):
                cols = pl.ds(side * FF + tile * i, tile)
                for k in range(4):
                    for n in range(2):
                        if k == 0:
                            src = (own, swapped)[n].at[pick, :, cols]
                        else:
                            src = got[3 * n + k - 1].at[:, cols]
                        dst = wbuf.at[buf, side, pl.ds((member ^ (k + 4 * n)) * 256, 256), :]
                        pltpu.make_async_copy(src, dst, sem.at[buf]).start()

        @pl.when(jnp.logical_not(active))
        def _():
            for side in range(2):
                cols = pl.ds(side * FF + tile * i, tile)
                pltpu.make_async_copy(slot.at[0, :, cols], wbuf.at[buf, side], sem.at[buf]).start()

    fetch(0)
    for i in range(3):
        if i < 2:
            fetch(i + 1)
        pltpu.make_async_copy(wbuf.at[i % 2], wbuf.at[i % 2], sem.at[i % 2]).wait()
        gate = nn_dot(x[...], wbuf[i % 2, 0])
        up = nn_dot(x[...], wbuf[i % 2, 1])
        hidden = gate / (1.0 + jnp.exp(-gate)) * up
        out[:, tile * i : tile * (i + 1)] = hidden.astype(BF16)


def down_kernel(ids, table, refreshed, h, own, swapped, *refs):
    got = refs[0:3]
    slot, out, wbuf, wide, packed, sem, sem_out = refs[3:]
    sends = []
    member = ids[1]
    active = member < ACTIVE
    pick = pick_of(ids, table, refreshed, member)
    order = (3, 0, 1, 2)

    @pl.when(active)
    def _():
        for j in order:
            cols = pl.ds(PART * j, PART)
            for k in range(4):
                for n in range(2):
                    if k == 0:
                        src = (own, swapped)[n].at[pick, :, cols]
                    else:
                        src = got[k - 1].at[n, :, cols]
                    dst = wbuf.at[j, pl.ds((member ^ (k + 4 * n)) * 96, 96), :]
                    pltpu.make_async_copy(src, dst, sem.at[j]).start()

    @pl.when(jnp.logical_not(active))
    def _():
        for j in order:
            cols = pl.ds(PART * j, PART)
            pltpu.make_async_copy(slot.at[0, :, cols], wbuf.at[j], sem.at[j]).start()

    for j in order:
        pltpu.make_async_copy(wbuf.at[j], wbuf.at[j], sem.at[j]).wait()
        y = nn_dot(h[...], wbuf[j])
        for r in range(CAP):
            part = y[128 * r : 128 * (r + 1)]
            at = r if j < 3 else 6 + r // 3
            left = PART * (j if j < 3 else r % 3)
            for c in range(0, PART, 128):
                tile = ROWS * ((left + c) // 128) + at
                wide[pl.ds(tile, 128, stride=8), :] = part[:, c : c + 128]
        if j < 3:
            for c in range(4 * j, 4 * (j + 1)):
                block = wide[ROWS * c : ROWS * (c + 1), :]
                left = 128 * (c - 4 * j)
                packed[j, :, left : left + 128] = block.astype(BF16)
            target = out.at[:, pl.ds(PART * j, PART)]
            sends.append(pltpu.make_async_copy(packed.at[j], target, sem_out.at[j]))
            sends[-1].start()
    for c in sends:
        c.wait()


def weigh_kernel(route, gate, out):
    home = home_of(route[...])
    gates = jnp.zeros((SLOTS, TOK), F32)
    for k in range(TOP):
        gates = jnp.where(hits_of(home, k), gate[k : k + 1, :], gates)
    high = gates.astype(BF16)
    low = (gates - high.astype(F32)).astype(BF16)
    eye = (iota((TOK, TOK), 0) == iota((TOK, TOK), 1)).astype(F32).astype(BF16)
    every = spread()
    wide, high, low = [
        nt_dot(nt_dot(eye, v).astype(BF16), every) for v in (ranks(home), high, low)
    ]
    place = (iota((TOK, ROWS), 1) & 7).astype(F32)
    masks = [(wide == place) & (place < CAP)]
    for j in range(3):
        wanted = jnp.where(place == 6, float(j), jnp.where(place == 7, float(3 + j), -2.0))
        masks.append(wide == wanted)
    for i, mask in enumerate(masks):
        out[i, 0:TOK, :] = jnp.where(mask, high, 0.0).astype(BF16)
        out[i, TOK:, :] = jnp.where(mask, low, 0.0).astype(BF16)


def combine_kernel(weight, y, out):
    tail = jnp.zeros((TOK, PART), F32)
    for j in range(3):
        part = y[:, PART * j : PART * (j + 1)]
        stack = jnp.concatenate([weight[0], weight[1 + j]], axis=0)
        got = nn_dot(stack, part)
        out[:, PART * j : PART * (j + 1)] = (got[0:TOK] + got[TOK : 2 * TOK]).astype(BF16)
        tail = tail + (got[2 * TOK : 3 * TOK] + got[3 * TOK :])
    out[:, WIDE:] = tail.astype(BF16)


def hbm(x):
    return pltpu.with_memory_space_constraint(x, pltpu.HBM)


def resident(x):
    return pltpu.with_memory_space_constraint(x, pltpu.VMEM)


def shape(*dims, dtype=BF16):
    return jax.ShapeDtypeStruct(dims, dtype)


def per_device(
    tokens,
    slot_route,
    route_gate,
    placement_table,
    refreshed,
    slot_gate_up,
    slot_down,
    new_gate_up,
    new_down,
):
    ids = jnp.stack([lax.axis_index(EP), lax.axis_index(DP)]).astype(jnp.int32)
    where = (ids, placement_table, refreshed)
    route = slot_route.T
    gate = route_gate.T

    def swap(x):
        return lax.ppermute(x, "zl", [(0, 1), (1, 0)])

    def move(x, k):
        return lax.ppermute(x, DP, [(d ^ k, d) for d in range(ACTIVE)])

    def stage(dims, *sources):
        count = len(sources)
        held = [2] * (count > 1) + list(dims)
        return pl.pallas_call(
            stage_kernel,
            out_shape=[pltpu.HBM(tuple(held), BF16)] * 3,
            in_specs=[SMEM] * 3 + [HBM] * count,
            out_specs=[HBM] * 3,
            scratch_shapes=[pltpu.VMEM((2, *dims), BF16)] * count
            + [pltpu.SemaphoreType.DMA((count,)), pltpu.SemaphoreType.DMA((3 * count,))],
            compiler_params=params(),
        )(*where, *[hbm(v) for v in sources])

    swapped_up = swap(new_gate_up)
    swapped_down = swap(new_down)
    marks = jnp.pad(slot_route.astype(BF16), ((0, 0), (0, 120)))
    packed = [jnp.concatenate([tokens, marks], axis=1)]
    for k in range(1, 4):
        packed.append(lax.ppermute(packed[0], "x", [(d ^ k, d) for d in range(4)]))
    own = stage((256, WIDE), new_gate_up)
    got_up = []
    for k in range(1, 4):
        got_up.append(move(own[k - 1], k))
    outgoing = pl.pallas_call(
        dispatch_kernel,
        out_shape=shape(32, 4, PACK, WIDE),
        in_specs=[SMEM] + [VMEM] * 4,
        out_specs=VMEM,
        compiler_params=params(),
        name="dispatch",
    )(ids, *[resident(p) for p in packed])
    incoming = lax.all_to_all(
        outgoing.reshape(32, 4 * PACK, WIDE), COLUMN, split_axis=0, concat_axis=0, tiled=True
    )
    incoming = resident(incoming.reshape(ROWS, WIDE))
    far = stage((256, WIDE), swapped_up)
    for k in range(1, 4):
        got_up.append(move(far[k - 1], k))
    both = stage((96, D), new_down, swapped_down)
    got_down = []
    for k in range(1, 4):
        got_down.append(move(both[k - 1], k))
    weight = pl.pallas_call(
        weigh_kernel,
        out_shape=pltpu.HBM((4, 2 * TOK, ROWS), BF16),
        in_specs=[VMEM, VMEM],
        out_specs=VMEM,
        compiler_params=params(),
        name="weigh",
    )(route, gate)
    rows = pl.pallas_call(
        compact_kernel,
        out_shape=pltpu.VMEM((DENSE, D), BF16),
        in_specs=[VMEM],
        out_specs=VMEM,
        compiler_params=params(),
        name="compact",
    )(incoming)
    hidden = pl.pallas_call(
        up_kernel,
        out_shape=pltpu.VMEM((DENSE, FF), BF16),
        in_specs=[SMEM] * 3 + [VMEM] + [HBM] * 9,
        out_specs=VMEM,
        scratch_shapes=[pltpu.VMEM((2, 2, D, 256), BF16), pltpu.SemaphoreType.DMA((2,))],
        compiler_params=params(28),
        name="up",
    )(*where, resident(rows), *[hbm(v) for v in (new_gate_up, swapped_up, *got_up, slot_gate_up)])
    results = pl.pallas_call(
        down_kernel,
        out_shape=pltpu.HBM((ROWS, WIDE), BF16),
        in_specs=[SMEM] * 3 + [VMEM] + [HBM] * 6,
        out_specs=HBM,
        scratch_shapes=[
            pltpu.VMEM((4, FF, PART), BF16),
            pltpu.VMEM((ROWS * WIDE // 128, 128), F32),
            pltpu.VMEM((3, ROWS, PART), BF16),
            pltpu.SemaphoreType.DMA((4,)),
            pltpu.SemaphoreType.DMA((3,)),
        ],
        compiler_params=params(28),
        name="down",
    )(*where, resident(hidden), *[hbm(v) for v in (new_down, swapped_down, *got_down, slot_down)])
    returned = lax.all_to_all(
        results.reshape(SLOTS, PACK, WIDE), EVERY, split_axis=0, concat_axis=0, tiled=True
    )
    returned = resident(returned.reshape(ROWS, WIDE))
    return pl.pallas_call(
        combine_kernel,
        out_shape=shape(TOK, D),
        in_specs=[VMEM, VMEM],
        out_specs=VMEM,
        compiler_params=params(),
        name="combine",
    )(hbm(weight), returned)


def solution(mesh):
    split = Mesh(mesh.devices.reshape(4, 2, 2, 2, 4), EVERY)
    return jax.shard_map(
        per_device,
        mesh=split,
        in_specs=(
            P(EVERY, None),
            P(EVERY, None),
            P(EVERY, None),
            P(),
            P(),
            P(EVERY, None, None),
            P(EVERY, None, None),
            P(EP, DP, None),
            P(EP, DP, None),
        ),
        out_specs=P(EVERY, None),
        check_vma=False,
    )
```

```python
import jax
import jax.numpy as jnp
from jax import lax
from jax.experimental import pallas as pl
from jax.experimental.pallas import tpu as pltpu
from jax.sharding import Mesh
from jax.sharding import PartitionSpec as P


D = 2048
FF = 768
TOP = 8
CAP = 6
TOK = 64
SLOTS = 128
ACTIVE = 6
PACK = 8
WIDE = 1536
PART = 512
EP = ("y", "zh", "core")
DP = ("zl", "x")
EVERY = EP + DP
COLUMN = EP + ("zl",)
ROWS = SLOTS * PACK
DENSE = SLOTS * CAP


HBM = pl.BlockSpec(memory_space=pltpu.HBM)
SMEM = pl.BlockSpec(memory_space=pltpu.SMEM)
VMEM = pl.BlockSpec(memory_space=pltpu.VMEM)
F32 = jnp.float32
BF16 = jnp.bfloat16


def params(mib=20):
    return pltpu.CompilerParams(vmem_limit_bytes=mib * 1024 * 1024)


def iota(shape, dim):
    return lax.broadcasted_iota(jnp.int32, shape, dim)


def nt_dot(a, b):
    return lax.dot_general(a, b, (((1,), (1,)), ((), ())), preferred_element_type=F32)


def nn_dot(a, b):
    return jnp.dot(a, b, preferred_element_type=F32)


def shift_of(member):
    return jnp.where(member < 4, member, jnp.where(member == 4, 8, jnp.where(member == 5, 15, 0)))


def home_of(slot):
    member = slot & 7
    return ((((slot >> 3) + shift_of(member)) & 15) << 3) | member


def pick_of(ids, table, refreshed, other):
    group = ids[0]
    slot = (((group - shift_of(other)) & 15) << 3) | other
    return (table[slot] == refreshed[2 * group + 1]).astype(jnp.int32)


def hits_of(home, k):
    return iota((SLOTS, TOK), 0) == home[k : k + 1, :]


def ranks(home):
    hits = jnp.zeros((SLOTS, TOK), F32)
    for k in range(TOP):
        hits = jnp.where(hits_of(home, k), 1.0, hits)
    before = (iota((TOK, TOK), 0) < iota((TOK, TOK), 1)).astype(F32).astype(BF16)
    rank = nn_dot(hits.astype(BF16), before)
    return jnp.where(hits > 0, rank, -1.0).astype(BF16)


def spread():
    return ((iota((ROWS, SLOTS), 0) >> 3) == iota((ROWS, SLOTS), 1)).astype(F32).astype(BF16)


def copy_all(pairs, sems):
    copies = [pltpu.make_async_copy(src, dst, sems.at[n]) for n, (src, dst) in enumerate(pairs)]
    for c in copies:
        c.start()
    for c in copies:
        c.wait()


def stage_kernel(ids, table, refreshed, *refs):
    if len(refs) == 5:
        picks = [pick_of(ids, table, refreshed, ids[1] ^ k) for k in range(1, 4)]
        copy_all([(refs[0].at[picks[k]], refs[1 + k]) for k in range(3)], refs[4])
        return
    count = (len(refs) - 5) // 2
    sources, outs, sem_in, sem_out = refs[:count], refs[count : count + 3], refs[-2], refs[-1]
    held = refs[count + 3 : -2]
    picks = [pick_of(ids, table, refreshed, ids[1] ^ k) for k in range(1, 4)]
    copy_all(list(zip(sources, held)), sem_in)
    copy_all(
        [
            (held[n].at[picks[k]], outs[k].at[n] if count > 1 else outs[k])
            for k in range(3)
            for n in range(count)
        ],
        sem_out,
    )


def dispatch_kernel(ids, *refs):
    routes, near, out = refs[:4], refs[4:8], refs[8]
    column = ids[1] & 3
    part = 32 * PACK
    every = (iota((part, SLOTS), 1) == 4 * (iota((part, SLOTS), 0) >> 3) + column).astype(F32)
    every = every.astype(BF16)
    place = (iota((part, SLOTS), 0) & 7).astype(F32)
    left = iota((part, SLOTS), 1) < TOK
    for k in range(4):
        rank = ranks(home_of(routes[k][...]))
        wide = nn_dot(every, jnp.concatenate([rank, rank], axis=1))
        main = left & (wide == place) & (place < CAP)
        for j in range(3):
            wanted = jnp.where(place == 6, float(j), jnp.where(place == 7, float(3 + j), -2.0))
            pick = (main | (jnp.logical_not(left) & (wide == wanted))).astype(F32).astype(BF16)
            cols = slice(PART * j, PART * (j + 1))
            rhs = jnp.concatenate([near[k][:, cols], near[k][:, WIDE:]], axis=0)
            got = nn_dot(pick, rhs).reshape(32, PACK, PART)
            out[:, column ^ k, :, cols] = got.astype(BF16)


def compact_kernel(x, out):
    row = iota((96, 128), 0)
    col = iota((96, 128), 1)
    rank = row >> 4
    base = (row & 15) * 8
    main = (col == base + rank).astype(F32).astype(BF16)
    extra = []
    for j in range(3):
        hit = (col == base + 6) & (rank == j) | (col == base + 7) & (rank == 3 + j)
        extra.append(hit.astype(F32).astype(BF16))
    extra = jnp.concatenate(extra, axis=1)
    for b in range(8):
        blk = x[128 * b : 128 * (b + 1), :]
        head = nn_dot(main, blk).astype(BF16)
        tall = jnp.concatenate([blk[:, PART * j : PART * (j + 1)] for j in range(3)], axis=0)
        tail = nn_dot(extra, tall).astype(BF16)
        for r in range(CAP):
            rows = slice(128 * r + 16 * b, 128 * r + 16 * (b + 1))
            out[rows, 0:WIDE] = head[16 * r : 16 * (r + 1)]
            out[rows, WIDE:] = tail[16 * r : 16 * (r + 1)]


def up_kernel(ids, table, refreshed, x, own, swapped, *refs):
    got = refs[0:6]
    slot, out, wbuf, sem = refs[6:]
    member = ids[1]
    active = member < ACTIVE
    pick = pick_of(ids, table, refreshed, member)
    tile = 256

    def fetch(i):
        buf = i % 2

        @pl.when(active)
        def _():
            for side in range(2):
                cols = pl.ds(side * FF + tile * i, tile)
                for k in range(4):
                    for n in range(2):
                        if k == 0:
                            src = (own, swapped)[n].at[pick, :, cols]
                        else:
                            src = got[3 * n + k - 1].at[:, cols]
                        dst = wbuf.at[buf, side, pl.ds((member ^ (k + 4 * n)) * 256, 256), :]
                        pltpu.make_async_copy(src, dst, sem.at[buf]).start()

        @pl.when(jnp.logical_not(active))
        def _():
            for side in range(2):
                cols = pl.ds(side * FF + tile * i, tile)
                pltpu.make_async_copy(slot.at[0, :, cols], wbuf.at[buf, side], sem.at[buf]).start()

    fetch(0)
    for i in range(3):
        if i < 2:
            fetch(i + 1)
        pltpu.make_async_copy(wbuf.at[i % 2], wbuf.at[i % 2], sem.at[i % 2]).wait()
        gate = nn_dot(x[...], wbuf[i % 2, 0])
        up = nn_dot(x[...], wbuf[i % 2, 1])
        hidden = gate / (1.0 + jnp.exp(-gate)) * up
        out[:, tile * i : tile * (i + 1)] = hidden.astype(BF16)


def down_kernel(ids, table, refreshed, h, own, swapped, *refs):
    got = refs[0:3]
    slot, out, wbuf, wide, packed, sem, sem_out = refs[3:]
    sends = []
    member = ids[1]
    active = member < ACTIVE
    pick = pick_of(ids, table, refreshed, member)
    order = (3, 0, 1, 2)

    @pl.when(active)
    def _():
        for j in order:
            cols = pl.ds(PART * j, PART)
            for k in range(4):
                for n in range(2):
                    if k == 0:
                        src = (own, swapped)[n].at[pick, :, cols]
                    else:
                        src = got[k - 1].at[n, :, cols]
                    dst = wbuf.at[j, pl.ds((member ^ (k + 4 * n)) * 96, 96), :]
                    pltpu.make_async_copy(src, dst, sem.at[j]).start()

    @pl.when(jnp.logical_not(active))
    def _():
        for j in order:
            cols = pl.ds(PART * j, PART)
            pltpu.make_async_copy(slot.at[0, :, cols], wbuf.at[j], sem.at[j]).start()

    for j in order:
        pltpu.make_async_copy(wbuf.at[j], wbuf.at[j], sem.at[j]).wait()
        y = nn_dot(h[...], wbuf[j])
        for r in range(CAP):
            part = y[128 * r : 128 * (r + 1)]
            at = r if j < 3 else 6 + r // 3
            left = PART * (j if j < 3 else r % 3)
            for c in range(0, PART, 128):
                tile = ROWS * ((left + c) // 128) + at
                wide[pl.ds(tile, 128, stride=8), :] = part[:, c : c + 128]
        if j < 3:
            for c in range(4 * j, 4 * (j + 1)):
                block = wide[ROWS * c : ROWS * (c + 1), :]
                left = 128 * (c - 4 * j)
                packed[j, :, left : left + 128] = block.astype(BF16)
            target = out.at[:, pl.ds(PART * j, PART)]
            sends.append(pltpu.make_async_copy(packed.at[j], target, sem_out.at[j]))
            sends[-1].start()
    for c in sends:
        c.wait()


def weigh_kernel(route, gate, out):
    home = home_of(route[...])
    gates = jnp.zeros((SLOTS, TOK), F32)
    for k in range(TOP):
        gates = jnp.where(hits_of(home, k), gate[k : k + 1, :], gates)
    high = gates.astype(BF16)
    low = (gates - high.astype(F32)).astype(BF16)
    eye = (iota((TOK, TOK), 0) == iota((TOK, TOK), 1)).astype(F32).astype(BF16)
    every = spread()
    wide, high, low = [
        nt_dot(nt_dot(eye, v).astype(BF16), every) for v in (ranks(home), high, low)
    ]
    place = (iota((TOK, ROWS), 1) & 7).astype(F32)
    masks = [(wide == place) & (place < CAP)]
    for j in range(3):
        wanted = jnp.where(place == 6, float(j), jnp.where(place == 7, float(3 + j), -2.0))
        masks.append(wide == wanted)
    for i, mask in enumerate(masks):
        out[i, 0:TOK, :] = jnp.where(mask, high, 0.0).astype(BF16)
        out[i, TOK:, :] = jnp.where(mask, low, 0.0).astype(BF16)


def combine_kernel(weight, y, out):
    tail = jnp.zeros((TOK, PART), F32)
    for j in range(3):
        part = y[:, PART * j : PART * (j + 1)]
        stack = jnp.concatenate([weight[0], weight[1 + j]], axis=0)
        got = nn_dot(stack, part)
        out[:, PART * j : PART * (j + 1)] = (got[0:TOK] + got[TOK : 2 * TOK]).astype(BF16)
        tail = tail + (got[2 * TOK : 3 * TOK] + got[3 * TOK :])
    out[:, WIDE:] = tail.astype(BF16)


def hbm(x):
    return pltpu.with_memory_space_constraint(x, pltpu.HBM)


def resident(x):
    return pltpu.with_memory_space_constraint(x, pltpu.VMEM)


def shape(*dims, dtype=BF16):
    return jax.ShapeDtypeStruct(dims, dtype)


def per_device(
    tokens,
    slot_route,
    route_gate,
    placement_table,
    refreshed,
    slot_gate_up,
    slot_down,
    new_gate_up,
    new_down,
):
    ids = jnp.stack([lax.axis_index(EP), lax.axis_index(DP)]).astype(jnp.int32)
    where = (ids, placement_table, refreshed)
    route = slot_route.T
    gate = route_gate.T

    def swap(x):
        return lax.ppermute(x, "zl", [(0, 1), (1, 0)])

    def move(x, k):
        return lax.ppermute(x, DP, [(d ^ k, d) for d in range(ACTIVE)])

    def stage_held(dims, source):
        return pl.pallas_call(
            stage_kernel,
            out_shape=[pltpu.HBM(dims, BF16)] * 3,
            in_specs=[SMEM] * 3 + [VMEM],
            out_specs=[HBM] * 3,
            scratch_shapes=[pltpu.SemaphoreType.DMA((3,))],
            compiler_params=params(),
        )(*where, resident(source))

    def stage(dims, *sources):
        count = len(sources)
        held = [2] * (count > 1) + list(dims)
        return pl.pallas_call(
            stage_kernel,
            out_shape=[pltpu.HBM(tuple(held), BF16)] * 3,
            in_specs=[SMEM] * 3 + [HBM] * count,
            out_specs=[HBM] * 3,
            scratch_shapes=[pltpu.VMEM((2, *dims), BF16)] * count
            + [pltpu.SemaphoreType.DMA((count,)), pltpu.SemaphoreType.DMA((3 * count,))],
            compiler_params=params(),
        )(*where, *[hbm(v) for v in sources])

    swapped_up = swap(new_gate_up)
    swapped_down = swap(new_down)
    near = [tokens]
    routes = [route]
    for k in range(1, 4):
        pairs = [(d ^ k, d) for d in range(4)]
        near.append(lax.ppermute(tokens, "x", pairs))
        routes.append(lax.ppermute(route, "x", pairs))
    own = stage((256, WIDE), new_gate_up)
    got_up = []
    for k in range(1, 4):
        got_up.append(move(own[k - 1], k))
    outgoing = pl.pallas_call(
        dispatch_kernel,
        out_shape=shape(32, 4, PACK, WIDE),
        in_specs=[SMEM] + [VMEM] * 8,
        out_specs=VMEM,
        compiler_params=params(),
        name="dispatch",
    )(ids, *routes, *[resident(p) for p in near])
    incoming = lax.all_to_all(
        outgoing.reshape(32, 4 * PACK, WIDE), COLUMN, split_axis=0, concat_axis=0, tiled=True
    )
    incoming = resident(incoming.reshape(ROWS, WIDE))
    far = stage_held((256, WIDE), swapped_up)
    for k in range(1, 4):
        got_up.append(move(far[k - 1], k))
    both = stage((96, D), new_down, swapped_down)
    got_down = []
    for k in range(1, 4):
        got_down.append(move(both[k - 1], k))
    weight = pl.pallas_call(
        weigh_kernel,
        out_shape=pltpu.HBM((4, 2 * TOK, ROWS), BF16),
        in_specs=[VMEM, VMEM],
        out_specs=VMEM,
        compiler_params=params(),
        name="weigh",
    )(route, gate)
    rows = pl.pallas_call(
        compact_kernel,
        out_shape=pltpu.VMEM((DENSE, D), BF16),
        in_specs=[VMEM],
        out_specs=VMEM,
        compiler_params=params(),
        name="compact",
    )(incoming)
    hidden = pl.pallas_call(
        up_kernel,
        out_shape=pltpu.VMEM((DENSE, FF), BF16),
        in_specs=[SMEM] * 3 + [VMEM] + [HBM] * 9,
        out_specs=VMEM,
        scratch_shapes=[pltpu.VMEM((2, 2, D, 256), BF16), pltpu.SemaphoreType.DMA((2,))],
        compiler_params=params(28),
        name="up",
    )(*where, resident(rows), *[hbm(v) for v in (new_gate_up, swapped_up, *got_up, slot_gate_up)])
    results = pl.pallas_call(
        down_kernel,
        out_shape=pltpu.HBM((ROWS, WIDE), BF16),
        in_specs=[SMEM] * 3 + [VMEM] + [HBM] * 6,
        out_specs=HBM,
        scratch_shapes=[
            pltpu.VMEM((4, FF, PART), BF16),
            pltpu.VMEM((ROWS * WIDE // 128, 128), F32),
            pltpu.VMEM((3, ROWS, PART), BF16),
            pltpu.SemaphoreType.DMA((4,)),
            pltpu.SemaphoreType.DMA((3,)),
        ],
        compiler_params=params(28),
        name="down",
    )(*where, resident(hidden), *[hbm(v) for v in (new_down, swapped_down, *got_down, slot_down)])
    returned = lax.all_to_all(
        results.reshape(SLOTS, PACK, WIDE), EVERY, split_axis=0, concat_axis=0, tiled=True
    )
    returned = resident(returned.reshape(ROWS, WIDE))
    return pl.pallas_call(
        combine_kernel,
        out_shape=shape(TOK, D),
        in_specs=[VMEM, VMEM],
        out_specs=VMEM,
        compiler_params=params(),
        name="combine",
    )(hbm(weight), returned)


def solution(mesh):
    split = Mesh(mesh.devices.reshape(4, 2, 2, 2, 4), EVERY)
    return jax.shard_map(
        per_device,
        mesh=split,
        in_specs=(
            P(EVERY, None),
            P(EVERY, None),
            P(EVERY, None),
            P(),
            P(),
            P(EVERY, None, None),
            P(EVERY, None, None),
            P(EP, DP, None),
            P(EP, DP, None),
        ),
        out_specs=P(EVERY, None),
        check_vma=False,
    )
```
